32 devices in a mesh: fsdp: 32 (over z, y, x, core).
Axes of the slice: x: 2, y: 2, z: 4, core: 2. Of those that a mesh axis runs over, the one named last changes fastest.
Arguments:
- hidden_in: bfloat16 [8192, 2560], P('fsdp'), may hold values from -6 to 6
- output_grad: bfloat16 [8192, 2560], P('fsdp'), may hold values from -6 to 6
- seq_lengths: int32 [32, 2], P('fsdp'), may hold values from 32 to 224, as said below
- deal_rows: int32 [32, 256], P('fsdp'), may hold values from 0 to 255, each once within a row
- input_gain: bfloat16 [2560], P('fsdp'), may hold values from 0.099609375 to 1.8984375
- query_down: bfloat16 [2560, 768], P('fsdp'), may hold values from -0.125 to 0.125
- query_gain: bfloat16 [768], P('fsdp'), may hold values from 0.099609375 to 1.8984375
- query_up: bfloat16 [768, 3840], P('fsdp'), may hold values from -0.21875 to 0.21875
- latent_down: bfloat16 [2560, 288], P('fsdp'), may hold values from -0.125 to 0.125
- latent_gain: bfloat16 [256], P('fsdp'), may hold values from 0.099609375 to 1.8984375
- latent_up: bfloat16 [256, 5120], P('fsdp'), may hold values from -0.375 to 0.375
- attention_out: bfloat16 [2560, 2560], P('fsdp'), may hold values from -4 to 4
- feed_gain: bfloat16 [2560], P('fsdp'), may hold values from 0.099609375 to 1.8984375
- feed_weights: bfloat16 [2560, 19200], P('fsdp'), may hold values from -1 to 1
Outputs:
- hidden_out: bfloat16 [8192, 2560], P('fsdp')
- input_grad: bfloat16 [8192, 2560], P('fsdp')
- input_gain_grad: float32 [2560], P('fsdp')
- query_down_grad: float32 [2560, 768], P('fsdp')
- query_gain_grad: float32 [768], P('fsdp')
- query_up_grad: float32 [768, 3840], P('fsdp')
- latent_down_grad: float32 [2560, 288], P('fsdp')
- latent_gain_grad: float32 [256], P('fsdp')
- latent_up_grad: float32 [256, 5120], P('fsdp')
- attention_out_grad: float32 [2560, 2560], P('fsdp')
- feed_gain_grad: float32 [2560], P('fsdp')
- feed_weights_grad: float32 [2560, 19200], P('fsdp')
The draws below stay inside these ranges and needn't reach their ends.
Inputs may be any that keep to these rules, and one draw needn't show every extreme that they name: `seq_lengths`: each pack's two lengths add up to 256. `deal_rows`: each device's row holds every number below 256 once.
All inputs are finite; a program needn't handle non-finite values.
Results may differ from the reference program's by a relative error of at most 0.02.
Values may be sent and summed in bfloat16 or wider, within the bound.
No kernel may reach another device: no remote copies, remote signals or barrier semaphores. Data moves between devices by JAX's collectives and lax.ppermute only.
A program may use at most 448 MiB of HBM per device.

```python
import math
import jax
import jax.numpy as jnp
from jax import lax

D = 2560
H = 40
DN = 64
DR = 32
DV = 64
QR = 768
KVR = 256
FF = 6400
TOK_DEV = 256
TOKENS = 8192
SHARE = 8
MINLEN = 32
N_FSDP = 32


def draw_seq_lengths(key, part):
    first_part = jax.random.randint(key, (N_FSDP,), MINLEN, TOK_DEV - MINLEN + 1)
    chosen = jax.random.randint(jax.random.fold_in(key, 7), (), 0, N_FSDP)
    first_part = jnp.where(jnp.arange(N_FSDP) == chosen, TOK_DEV - MINLEN, first_part)
    return jnp.stack([first_part, TOK_DEV - first_part], axis=1).astype(jnp.int32)


def draw_feed_weights(key, part):
    column = jnp.arange(3 * FF)
    factor = jnp.where(column < 2 * FF, 1.0 / math.sqrt(D), 1.0 / math.sqrt(FF / 100.0))
    limit = jnp.minimum(6.0, 1.0 / factor)
    values = jax.random.normal(key, (D, 3 * FF), jnp.float32)
    values = jnp.clip(values, -limit[None, :], limit[None, :])
    return (values * factor[None, :]).astype(jnp.bfloat16)


def steps_of(stream_key, shape, cuts, low, top_value):
    def one(dim, parts):
        heights = jax.random.uniform(jax.random.fold_in(jax.random.fold_in(stream_key, 6), dim), (parts,), jnp.float32, low / len(cuts), top_value / len(cuts))
        return jnp.repeat(jnp.exp(heights), shape[dim] // parts).reshape((-1,) + (1,) * (len(shape) - dim - 1))

    loudness = one(*cuts[0])
    for cut in cuts[1:]:
        loudness = loudness * one(*cut)
    return loudness


def scatter_about(key, dims, deviation, bound, split=(), kind=jnp.bfloat16):
    values = deviation * jax.random.normal(key, dims, jnp.float32)
    if split:
        values = values * steps_of(key, dims, split, -0.22, 0.18)
    return jnp.clip(values, -bound, bound).astype(kind)


def setup_inputs(seed: int = 0) -> dict:
    splits = jax.random.split(jax.random.key(seed), 15)
    return {
        "hidden_in": scatter_about(splits[0], (TOKENS, D), 1.0, 6.0, ((0, 32),)),
        "output_grad": scatter_about(splits[1], (TOKENS, D), 1.0, 6.0, ((0, 32),)),
        "seq_lengths": draw_seq_lengths(jax.random.fold_in(splits[14], 71), 0),
        "deal_rows": jax.vmap(lambda own: jax.random.permutation(own, TOK_DEV))(jax.random.split(splits[3], N_FSDP)).reshape((N_FSDP, TOK_DEV)).astype(jnp.int32),
        "input_gain": jnp.clip(1.0 + 0.18 * jax.random.normal(splits[4], (D,), jnp.float32), 0.099609375, 1.8984375).astype(jnp.bfloat16),
        "query_down": scatter_about(splits[5], (D, QR), D ** -0.5, 0.125, ((0, 32),)),
        "query_gain": jnp.clip(1.0 + 0.18 * jax.random.normal(splits[6], (QR,), jnp.float32), 0.099609375, 1.8984375).astype(jnp.bfloat16),
        "query_up": scatter_about(splits[7], (QR, H * (DN + DR)), QR ** -0.5, 0.21875, ((0, 32),)),
        "latent_down": scatter_about(splits[8], (D, KVR + DR), D ** -0.5, 0.125, ((0, 32),)),
        "latent_gain": jnp.clip(1.0 + 0.18 * jax.random.normal(splits[9], (KVR,), jnp.float32), 0.099609375, 1.8984375).astype(jnp.bfloat16),
        "latent_up": scatter_about(splits[10], (KVR, H * (DN + DV)), KVR ** -0.5, 0.375, ((0, 32),)),
        "attention_out": scatter_about(splits[11], (H * DV, D), 2 ** -0.5, 4.0, ((0, 32),)),
        "feed_gain": jnp.clip(1.0 + 0.18 * jax.random.normal(splits[12], (D,), jnp.float32), 0.099609375, 1.8984375).astype(jnp.bfloat16),
        "feed_weights": draw_feed_weights(jax.random.fold_in(splits[14], 71), 0),
    }


EPS = 1e-05
RESID = 1.4 / math.sqrt(62.0)
HIGH = lax.Precision.HIGHEST

@jax.custom_vjp
def low(v):
    return lax.optimization_barrier(v.astype(jnp.bfloat16)).astype(jnp.float32)

@jax.custom_vjp
def low_back(v):
    return v

def low_keep(v):
    return (low(v), None)

def low_pass(kept, grad):
    return (grad,)

def back_keep(v):
    return (v, None)

def back_low(kept, grad):
    return (low(grad),)
low.defvjp(low_keep, low_pass)
low_back.defvjp(back_keep, back_low)

def normed(value):
    return value * lax.rsqrt(lax.optimization_barrier(jnp.mean(value * value, axis=-1, keepdims=True)) + EPS)

def rotary_tables(position):
    halves = DR // 2
    frequency = jnp.exp(jnp.arange(halves, dtype=jnp.float32) * (-2.0 * math.log(10000.0) / DR))
    angle = position.astype(jnp.float32)[:, None] * frequency[None, :]
    return (jnp.cos(angle), jnp.sin(angle))

def rotate(value, cosine, sine):
    halves = cosine.shape[-1]
    first_half = value[..., :halves]
    second_half = value[..., halves:]
    return jnp.concatenate([first_half * cosine - second_half * sine, second_half * cosine + first_half * sine], axis=-1)

def allowed_pairs(first_length):
    index_rows = jnp.arange(TOK_DEV)
    segment = index_rows >= first_length
    return (segment[:, None] == segment[None, :]) & (index_rows[None, :] <= index_rows[:, None])

def pack_attention(block):
    queries, keys, values, first_length = block
    scores = low_back(jnp.einsum('qhd,khd->hqk', queries, keys, precision=HIGH))
    masked = jnp.where(allowed_pairs(first_length)[None], scores, -1e+30)
    peak = lax.optimization_barrier(jnp.max(masked, axis=-1, keepdims=True))
    expo = jnp.exp(masked - peak)
    prob = expo / lax.optimization_barrier(jnp.sum(expo, axis=-1, keepdims=True))
    return jnp.einsum('hqk,khd->qhd', low(prob), values, precision=HIGH)

def layer(dealt, input_gain, query_down, query_gain, query_up, latent_down, latent_gain, latent_up, attention_out, feed_gain, feed_weights, cosine, sine, first_lengths):
    count_rows = dealt.shape[0]
    packs = count_rows // TOK_DEV
    factor = 1.0 / math.sqrt(DN + DR)
    h_one = low(normed(dealt) * input_gain)
    q_low = low_back(jnp.dot(h_one, query_down, precision=HIGH))
    q_normed = low(normed(q_low) * query_gain)
    q_full = low_back(jnp.dot(q_normed, query_up, precision=HIGH)).reshape(count_rows, H, DN + DR)
    q_rope = rotate(q_full[..., DN:], cosine[:, None, :], sine[:, None, :])
    queries = low(factor * jnp.concatenate([q_full[..., :DN], q_rope], axis=-1))
    kv_low = low_back(jnp.dot(h_one, latent_down, precision=HIGH))
    l_normed = low(normed(kv_low[:, :KVR]) * latent_gain)
    kv_full = low(low_back(jnp.dot(l_normed, latent_up, precision=HIGH))).reshape(count_rows, H, DN + DV)
    k_rope = low(rotate(kv_low[:, KVR:], cosine, sine))
    keys = jnp.concatenate([kv_full[..., :DN], jnp.broadcast_to(k_rope[:, None, :], (count_rows, H, DR))], axis=-1)
    values = kv_full[..., DN:]
    mixed = lax.map(jax.checkpoint(pack_attention), (queries.reshape(packs, TOK_DEV, H, DN + DR), keys.reshape(packs, TOK_DEV, H, DN + DR), values.reshape(packs, TOK_DEV, H, DV), first_lengths))
    attended = low(low_back(mixed.reshape(count_rows, H * DV)))
    branch = low_back(jnp.dot(attended, attention_out, precision=HIGH))
    middle = dealt + RESID * branch
    h_two = low(normed(middle) * feed_gain)
    gate_up = low_back(jnp.dot(h_two, feed_weights[:, :2 * FF], precision=HIGH))
    inner = low(jax.nn.silu(gate_up[:, :FF]) * gate_up[:, FF:])
    feed = low_back(jnp.dot(inner, feed_weights[:, 2 * FF:].T, precision=HIGH))
    return middle + RESID * feed

def reference(hidden_in, output_grad, seq_lengths, deal_rows, input_gain, query_down, query_gain, query_up, latent_down, latent_gain, latent_up, attention_out, feed_gain, feed_weights):
    target = jnp.arange(N_FSDP).reshape(N_FSDP, 1, 1)
    slot_index = jnp.arange(SHARE).reshape(1, SHARE, 1)
    sender = jnp.arange(N_FSDP).reshape(1, 1, N_FSDP)
    source = (sender * TOK_DEV + deal_rows[sender, target * SHARE + slot_index]).reshape(TOKENS).astype(jnp.int32)
    dealt = hidden_in[source].astype(jnp.float32)
    cotangent = output_grad[source].astype(jnp.float32)
    first_lengths = seq_lengths[:, 0].astype(jnp.int32)
    index_rows = jnp.arange(TOKENS) % TOK_DEV
    first_row = jnp.repeat(first_lengths, TOK_DEV)
    position = jnp.where(index_rows >= first_row, index_rows - first_row, index_rows)
    cosine, sine = rotary_tables(position)

    def forward(dealt_in, g_in, w_qd, g_q, w_qu, w_ld, g_l, w_lu, w_out, g_mid, w_feed):
        return layer(dealt_in, g_in, w_qd, g_q, w_qu, w_ld, g_l, w_lu, w_out, g_mid, w_feed, cosine, sine, first_lengths)
    result, pull = jax.vjp(forward, dealt, input_gain.astype(jnp.float32), query_down.astype(jnp.float32), query_gain.astype(jnp.float32), query_up.astype(jnp.float32), latent_down.astype(jnp.float32), latent_gain.astype(jnp.float32), latent_up.astype(jnp.float32), attention_out.astype(jnp.float32), feed_gain.astype(jnp.float32), feed_weights.astype(jnp.float32))
    grads = pull(cotangent)

    def undeal(value):
        return jnp.zeros_like(value).at[source].set(value)
    return (undeal(result).astype(jnp.bfloat16), undeal(grads[0]).astype(jnp.bfloat16), grads[1], grads[2], grads[3], grads[4], grads[5], grads[6], grads[7], grads[8], grads[9], grads[10])
```

```python
import math

import jax
import jax.numpy as jnp
from jax import lax
from jax.sharding import PartitionSpec as P

H = 40
DN = 64
DR = 32
DV = 64
KVR = 256
FF = 6400


EPS = 1e-05
RESID = 1.4 / math.sqrt(62.0)
NEGATIVE = -1e30
NEAR = 8


def normed(value):
    inverse = lax.rsqrt(jnp.mean(value * value, axis=-1, keepdims=True) + EPS)
    return (value * inverse, inverse)


def norm_back(unit, inverse, incoming):
    return inverse * (incoming - unit * jnp.mean(incoming * unit, axis=-1, keepdims=True))


def rotary_tables(position):
    halves = DR // 2
    frequency = jnp.exp(jnp.arange(halves, dtype=jnp.float32) * (-2.0 * math.log(10000.0) / DR))
    angle = position.astype(jnp.float32)[:, None] * frequency[None, :]
    return (jnp.cos(angle), jnp.sin(angle))


def rotate(value, cosine, sine):
    halves = cosine.shape[-1]
    first_half = value[..., :halves]
    second_half = value[..., halves:]
    return jnp.concatenate(
        [first_half * cosine - second_half * sine, second_half * cosine + first_half * sine],
        axis=-1,
    )


def rotate_back(incoming, cosine, sine):
    halves = cosine.shape[-1]
    first_half = incoming[..., :halves]
    second_half = incoming[..., halves:]
    return jnp.concatenate(
        [first_half * cosine + second_half * sine, second_half * cosine - first_half * sine],
        axis=-1,
    )


def dot_plain(left, right):
    return jnp.dot(left, right, preferred_element_type=jnp.float32)


def dot_rows(left, right):
    return lax.dot_general(
        left, right, (((0,), (0,)), ((), ())), preferred_element_type=jnp.float32
    )


def dot_last(left, right):
    return lax.dot_general(
        left, right, (((1,), (1,)), ((), ())), preferred_element_type=jnp.float32
    )


def given_order(received, deal_order, devices, share):
    flat = received.reshape(devices * share, received.shape[-1])
    inverse = jnp.argsort(deal_order)
    pick = inverse % share * devices + inverse // share
    return flat[pick]


def move_near(value, devices, mask):
    return lax.ppermute(value, "fsdp", [(d, d ^ mask) for d in range(devices)])


def move_far(value, devices, step):
    return lax.ppermute(value, "fsdp", [(d, (d + NEAR * step) % devices) for d in range(devices)])


def near_slots(value, devices):
    across = {mask: move_near(value, devices, mask) for mask in (2, 4, 6)}
    slots = [value, move_near(value, devices, 1)]
    for mask in (2, 4, 6):
        slots += [across[mask], move_near(across[mask], devices, 1)]
    return slots


def far_slots(value, devices):
    slots = [value]
    for _ in range(devices // NEAR - 1):
        slots.append(move_far(slots[-1], devices, -1))
    return slots


def far_gather(value, devices, group):
    far = devices // NEAR
    out = jnp.zeros((far,) + value.shape, value.dtype)
    for k, slot in enumerate(far_slots(value, devices)):
        out = lax.dynamic_update_slice_in_dim(out, slot[None], (group + k) % far, 0)
    return out


def gather_all(value, devices, group, member):
    lines = far_gather(value, devices, group)
    out = jnp.zeros((devices // NEAR, NEAR) + value.shape, value.dtype)
    for j, slot in enumerate(near_slots(lines, devices)):
        out = lax.dynamic_update_slice_in_dim(out, slot[:, None], member ^ j, 1)
    return out.reshape((devices * value.shape[0],) + value.shape[1:])


def near_scatter(slots, devices):
    low = [s.astype(jnp.bfloat16) for s in slots]
    paired = [
        slots[j].astype(jnp.float32) + move_near(low[j + 1], devices, 1).astype(jnp.float32)
        for j in (0, 2, 4, 6)
    ]
    total = paired[0]
    for index, mask in ((1, 2), (2, 4), (3, 6)):
        total = total + move_near(paired[index].astype(jnp.bfloat16), devices, mask).astype(jnp.float32)
    return total


def far_scatter(slots, devices):
    total = slots[-1].astype(jnp.float32)
    for slot in slots[-2::-1]:
        total = move_far(total.astype(jnp.bfloat16), devices, 1).astype(jnp.float32) + slot.astype(jnp.float32)
    return total


def scatter_all(term, devices, group, member):
    far = devices // NEAR
    rows = term.shape[0] // devices
    parts = term.reshape((far, NEAR, rows) + term.shape[1:])
    slots = [lax.dynamic_index_in_dim(parts, member ^ j, 1, keepdims=False) for j in range(NEAR)]
    lines = near_scatter(slots, devices)
    return far_scatter(
        [lax.dynamic_index_in_dim(lines, (group + k) % far, 0, keepdims=False) for k in range(far)],
        devices,
    )


def near_groups(devices):
    return [list(range(start, start + NEAR)) for start in range(0, devices, NEAR)]


def hidden_columns(block, devices, group):
    rows, width = block.shape
    pieces = block.reshape(rows, NEAR, width // NEAR).transpose(1, 0, 2)
    mine = lax.all_to_all(
        pieces, "fsdp", split_axis=0, concat_axis=0, tiled=True, axis_index_groups=near_groups(devices)
    ).reshape(NEAR * rows, width // NEAR)
    return far_gather(mine, devices, group).reshape(devices * rows, width // NEAR)


def hidden_columns_sum(term, devices, group):
    far = devices // NEAR
    rows, width = term.shape[0] // devices, term.shape[1]
    parts = term.reshape(far, NEAR * rows, width)
    mine = far_scatter(
        [lax.dynamic_index_in_dim(parts, (group + k) % far, 0, keepdims=False) for k in range(far)],
        devices,
    )
    pieces = lax.all_to_all(
        mine.astype(jnp.bfloat16).reshape(NEAR, rows, width),
        "fsdp",
        split_axis=0,
        concat_axis=0,
        tiled=True,
        axis_index_groups=near_groups(devices),
    )
    return pieces.transpose(1, 0, 2).reshape(rows, NEAR * width).astype(jnp.float32)


def probabilities(queries, keys, allowed, log_total):
    scores = jnp.einsum("qhd,khd->hqk", queries, keys, preferred_element_type=jnp.float32)
    masked = jnp.where(allowed[None], scores, NEGATIVE)
    return jnp.exp(masked - log_total)


def per_device(
    hidden_in,
    output_grad,
    seq_lengths,
    deal_rows,
    input_gain,
    query_down,
    query_gain,
    query_up,
    latent_down,
    latent_gain,
    latent_up,
    attention_out,
    feed_gain,
    feed_weights,
):
    devices = lax.axis_size("fsdp")
    place = lax.axis_index("fsdp")
    group, member = place // NEAR, place % NEAR
    count_rows = hidden_in.shape[0]
    model_width = hidden_in.shape[1]
    share = count_rows // devices
    owned = query_down.shape[0]
    q_rank, q_owned = query_down.shape[1], query_up.shape[0]
    l_owned = latent_up.shape[0]
    deal_order = deal_rows[0]
    order_table = deal_order.reshape(devices, share).T
    dealt_in, dealt_grad = (
        lax.all_to_all(hidden_in[order_table], "fsdp", split_axis=1, concat_axis=1, tiled=True),
        lax.all_to_all(output_grad[order_table], "fsdp", split_axis=1, concat_axis=1, tiled=True),
    )
    dealt_in = dealt_in.reshape(count_rows, model_width).astype(jnp.float32)
    dealt_grad = dealt_grad.reshape(count_rows, model_width).astype(jnp.float32)

    low_gains = jnp.zeros((owned,), jnp.bfloat16)
    low_gains = low_gains.at[:q_owned].set(query_gain)
    low_gains = low_gains.at[q_owned : q_owned + l_owned].set(latent_gain)
    down_set = jnp.concatenate(
        [query_down, latent_down, input_gain[:, None], feed_gain[:, None], low_gains[:, None]], axis=1
    )
    down_all = gather_all(down_set, devices, group, member)
    down_width = q_rank + KVR + DR
    w_qd = down_all[:, :q_rank]
    w_ld = down_all[:, q_rank:down_width]
    g_in = down_all[:, down_width]
    g_mid = down_all[:, down_width + 1]
    g_low = down_all[:, down_width + 2].reshape(devices, owned)
    g_q = g_low[:, :q_owned].reshape(-1)
    g_l = g_low[:, q_owned : q_owned + l_owned].reshape(-1)
    w_qu = gather_all(query_up, devices, group, member)
    w_lu = gather_all(latent_up, devices, group, member)
    w_out = gather_all(attention_out, devices, group, member)
    w_gate = hidden_columns(feed_weights[:, :FF], devices, group)
    w_up = hidden_columns(feed_weights[:, FF : 2 * FF], devices, group)
    w_down = hidden_columns(feed_weights[:, 2 * FF :], devices, group)

    index_rows = jnp.arange(count_rows)
    first_length = seq_lengths[0, 0]
    segment = index_rows >= first_length
    allowed = (segment[:, None] == segment[None, :]) & (index_rows[None, :] <= index_rows[:, None])
    position = jnp.where(segment, index_rows - first_length, index_rows)
    cosine, sine = rotary_tables(position)
    head_cos = cosine[:, None, :]
    head_sin = sine[:, None, :]
    factor = 1.0 / math.sqrt(DN + DR)
    unit_in, inv_in = normed(dealt_in)
    h_one = (unit_in * g_in.astype(jnp.float32)).astype(jnp.bfloat16)
    q_low = dot_plain(h_one, w_qd)
    unit_q, inv_q = normed(q_low)
    q_normed = (unit_q * g_q.astype(jnp.float32)).astype(jnp.bfloat16)
    q_full = dot_plain(q_normed, w_qu).reshape(count_rows, H, DN + DR)
    q_rope = rotate(q_full[..., DN:], head_cos, head_sin)
    queries = (factor * jnp.concatenate([q_full[..., :DN], q_rope], axis=-1)).astype(jnp.bfloat16)
    kv_low = dot_plain(h_one, w_ld)
    unit_l, inv_l = normed(kv_low[:, :KVR])
    l_normed = (unit_l * g_l.astype(jnp.float32)).astype(jnp.bfloat16)
    kv_full = dot_plain(l_normed, w_lu).astype(jnp.bfloat16).reshape(count_rows, H, DN + DV)
    k_rope = rotate(kv_low[:, KVR:], cosine, sine).astype(jnp.bfloat16)
    keys = jnp.concatenate(
        [kv_full[..., :DN], jnp.broadcast_to(k_rope[:, None, :], (count_rows, H, DR))], axis=-1
    )
    values = kv_full[..., DN:]
    scores = jnp.einsum("qhd,khd->hqk", queries, keys, preferred_element_type=jnp.float32)
    masked = jnp.where(allowed[None], scores, NEGATIVE)
    peak = jnp.max(masked, axis=-1, keepdims=True)
    log_total = peak + jnp.log(jnp.sum(jnp.exp(masked - peak), axis=-1, keepdims=True))
    prob = jnp.exp(masked - log_total)
    mixed = jnp.einsum(
        "hqk,khd->qhd", prob.astype(jnp.bfloat16), values, preferred_element_type=jnp.float32
    )
    attended = mixed.reshape(count_rows, H * DV).astype(jnp.bfloat16)
    middle = dealt_in + RESID * dot_plain(attended, w_out)
    unit_mid, inv_mid = normed(middle)
    h_two = (unit_mid * g_mid.astype(jnp.float32)).astype(jnp.bfloat16)

    h_all = jnp.concatenate(near_slots(h_two, devices), axis=0)
    d_feed = (RESID * dealt_grad).astype(jnp.bfloat16)
    d_all = jnp.concatenate(near_slots(d_feed, devices), axis=0)
    gate_part = dot_plain(h_all, w_gate)
    up_part = dot_plain(h_all, w_up)
    sigma = jax.nn.sigmoid(gate_part)
    active = gate_part * sigma
    inner = (active * up_part).astype(jnp.bfloat16)
    d_inner = dot_plain(d_all, w_down)
    d_gate = (d_inner * up_part * sigma * (1.0 + gate_part * (1.0 - sigma))).astype(jnp.bfloat16)
    d_up = (d_inner * active).astype(jnp.bfloat16)
    d_h_terms = dot_last(d_gate, w_gate) + dot_last(d_up, w_up)
    d_h_two = near_scatter(list(d_h_terms.reshape(NEAR, count_rows, model_width)), devices)
    result_terms = dot_last(inner, w_down)
    feed_out = near_scatter(list(result_terms.reshape(NEAR, count_rows, model_width)), devices)
    result = middle + RESID * feed_out
    back_rows = result.astype(jnp.bfloat16).reshape(share, devices, model_width)
    returned = lax.all_to_all(back_rows, "fsdp", split_axis=1, concat_axis=1, tiled=True)
    hidden_out = given_order(returned, deal_order, devices, share)
    feed_weights_grad = jnp.concatenate(
        [
            hidden_columns_sum(dot_rows(h_all, d_gate), devices, group),
            hidden_columns_sum(dot_rows(h_all, d_up), devices, group),
            hidden_columns_sum(dot_rows(d_all, inner), devices, group),
        ],
        axis=1,
    )

    d_g_mid = jnp.sum(d_h_two * unit_mid, axis=0)
    d_middle = dealt_grad + norm_back(unit_mid, inv_mid, d_h_two * g_mid.astype(jnp.float32))
    d_branch = (RESID * d_middle).astype(jnp.bfloat16)
    d_w_out = dot_rows(attended, d_branch)
    d_attended = dot_last(d_branch, w_out).astype(jnp.bfloat16).reshape(count_rows, H, DV)
    prob_again = probabilities(queries, keys, allowed, log_total)
    d_prob = jnp.einsum("qhd,khd->hqk", d_attended, values, preferred_element_type=jnp.float32)
    d_values = jnp.einsum(
        "hqk,qhd->khd",
        prob_again.astype(jnp.bfloat16),
        d_attended,
        preferred_element_type=jnp.float32,
    )
    row_sums = jnp.sum(d_prob * prob_again, axis=-1, keepdims=True)
    d_scores = (prob_again * (d_prob - row_sums)).astype(jnp.bfloat16)
    d_queries = jnp.einsum("hqk,khd->qhd", d_scores, keys, preferred_element_type=jnp.float32)
    d_keys = jnp.einsum("hqk,qhd->khd", d_scores, queries, preferred_element_type=jnp.float32)
    d_q_rope = rotate_back(d_queries[..., DN:], head_cos, head_sin)
    d_q_full = (
        (factor * jnp.concatenate([d_queries[..., :DN], d_q_rope], axis=-1))
        .reshape(count_rows, H * (DN + DR))
        .astype(jnp.bfloat16)
    )
    d_w_qu = dot_rows(q_normed, d_q_full)
    d_q_normed = dot_last(d_q_full, w_qu)
    d_g_q = jnp.sum(d_q_normed * unit_q, axis=0)
    d_q_low = norm_back(unit_q, inv_q, d_q_normed * g_q.astype(jnp.float32)).astype(jnp.bfloat16)
    d_kv_full = (
        jnp.concatenate([d_keys[..., :DN], d_values], axis=-1)
        .reshape(count_rows, H * (DN + DV))
        .astype(jnp.bfloat16)
    )
    d_w_lu = dot_rows(l_normed, d_kv_full)
    d_l_normed = dot_last(d_kv_full, w_lu)
    d_g_l = jnp.sum(d_l_normed * unit_l, axis=0)
    d_latent = norm_back(unit_l, inv_l, d_l_normed * g_l.astype(jnp.float32))
    d_k_rope = rotate_back(jnp.sum(d_keys[..., DN:], axis=1), cosine, sine)
    d_kv_low = jnp.concatenate([d_latent, d_k_rope], axis=1).astype(jnp.bfloat16)
    d_w_ld = dot_rows(h_one, d_kv_low)
    d_w_qd = dot_rows(h_one, d_q_low)
    d_h_one = dot_last(d_q_low, w_qd) + dot_last(d_kv_low, w_ld)
    d_g_in = jnp.sum(d_h_one * unit_in, axis=0)
    d_input = d_middle + norm_back(unit_in, inv_in, d_h_one * g_in.astype(jnp.float32))
    grad_rows = d_input.astype(jnp.bfloat16).reshape(share, devices, model_width)
    grad_returned = lax.all_to_all(grad_rows, "fsdp", split_axis=1, concat_axis=1, tiled=True)
    input_grad = given_order(grad_returned, deal_order, devices, share)

    d_low_gains = jnp.concatenate(
        [
            d_g_q.reshape(devices, q_owned),
            d_g_l.reshape(devices, l_owned),
            jnp.zeros((devices, owned - q_owned - l_owned), jnp.float32),
        ],
        axis=1,
    ).reshape(-1)
    out_sum = scatter_all(d_w_out, devices, group, member)
    query_up_sum = scatter_all(d_w_qu, devices, group, member)
    latent_up_sum = scatter_all(d_w_lu, devices, group, member)
    d_down_set = jnp.concatenate(
        [d_w_qd, d_w_ld, d_g_in[:, None], d_g_mid[:, None], d_low_gains[:, None]], axis=1
    )
    down_sum = scatter_all(d_down_set, devices, group, member)
    low_sum = down_sum[:, down_width + 2]
    return (
        hidden_out,
        input_grad,
        down_sum[:, down_width],
        down_sum[:, :q_rank],
        low_sum[:q_owned],
        query_up_sum,
        down_sum[:, q_rank:down_width],
        low_sum[q_owned : q_owned + l_owned],
        latent_up_sum,
        out_sum,
        down_sum[:, down_width + 1],
        feed_weights_grad,
    )


def solution(mesh):
    placed = (
        P("fsdp", None),
        P("fsdp", None),
        P("fsdp", None),
        P("fsdp", None),
        P("fsdp"),
        P("fsdp", None),
        P("fsdp"),
        P("fsdp", None),
        P("fsdp", None),
        P("fsdp"),
        P("fsdp", None),
        P("fsdp", None),
        P("fsdp"),
        P("fsdp", None),
    )
    return jax.shard_map(
        per_device,
        mesh=mesh,
        in_specs=placed,
        out_specs=(
            P("fsdp", None),
            P("fsdp", None),
            P("fsdp"),
            P("fsdp", None),
            P("fsdp"),
            P("fsdp", None),
            P("fsdp", None),
            P("fsdp"),
            P("fsdp", None),
            P("fsdp", None),
            P("fsdp"),
            P("fsdp", None),
        ),
        check_vma=False,
    )
```
